32 devices in a mesh: row: 16 (over z, y, x), col: 2 (over core).
Axes of the slice: x: 2, y: 2, z: 4, core: 2. Of those that a mesh axis runs over, the one named last changes fastest.
Arguments:
- panel: bfloat16 [65536, 256], P('row'), may hold values from -400 to 400, as said below
- slab: bfloat16 [65536, 1024], P('row', 'col'), may hold values from -300 to 300
Outputs:
- factor: float32 [256, 256], P(None, 'col')
- coupling: float32 [256, 1024], P(None, 'col')
- remainder: bfloat16 [65536, 1024], P('row', 'col')
The draws below stay inside these ranges and needn't reach their ends.
Inputs may be any that keep to these rules, and one draw needn't show every extreme that they name: panel has full column rank.
All inputs are finite; a program needn't handle non-finite values.
Results may differ from the reference program's by a relative error of at most 0.015.
The reference program's roundings to bfloat16 on the way (of `update`) count: a program that leaves them out, or rounds other values in their place, can miss the bound.
Values sent between devices are 32-bit elements; how exact they have to be, the bound alone decides.
A program may use at most 64 MiB of HBM per device.

```python
import jax
import jax.numpy as jnp
from jax import lax

K = 256
SLAB = 1024
M = 65536


def panel_values(key):
    base = jax.random.fold_in(key, 7)
    keys = jax.random.split(base, 3)
    raw = jax.random.normal(keys[0], (M, K), jnp.float32)
    mixing = jnp.eye(K, dtype=jnp.float32) + 0.5 * jax.random.normal(keys[1], (K, K), jnp.float32) / jnp.sqrt(K * 1.0)
    column_scale = jnp.exp(jax.random.uniform(keys[2], (K,), jnp.float32, jnp.log(0.5), jnp.log(2.0)))
    trend = 1.0 + 2.0 * jnp.arange(M, dtype=jnp.float32) / M
    row_scale = trend
    values = jnp.dot(raw, mixing) * column_scale[None, :] * row_scale[:, None]
    return jnp.clip(values, -400.0, 400.0)


def draw_panel(key, part):
    return panel_values(key).astype(jnp.bfloat16)


def draw_slab(key, part):
    values = panel_values(key)
    keys = jax.random.split(jax.random.fold_in(key, 13), 2)
    mixing = jax.random.normal(keys[0], (K, SLAB), jnp.float32) / jnp.sqrt(K * 1.0)
    noise = 0.5 * jax.random.normal(keys[1], (M, SLAB), jnp.float32)
    return jnp.clip(jnp.dot(values, mixing) + noise, -300.0, 300.0).astype(jnp.bfloat16)


def setup_inputs(seed: int = 0) -> dict:
    streams_of = jax.random.split(jax.random.key(seed), 3)
    return {
        "panel": draw_panel(jax.random.fold_in(streams_of[2], 71), 0),
        "slab": draw_slab(jax.random.fold_in(streams_of[2], 71), 0),
    }


def reference(panel, slab):
    total_rows = panel.shape[0]
    wide_panel = panel.astype(jnp.float32)
    wide_slab = slab.astype(jnp.float32)
    gram = jnp.dot(wide_panel.T, wide_panel, precision=lax.Precision.HIGHEST) / total_rows
    factor = jnp.linalg.cholesky(gram).T
    cross = jnp.dot(wide_panel.T, wide_slab, precision=lax.Precision.HIGHEST) / total_rows
    coupling = lax.linalg.triangular_solve(factor, cross, left_side=True, lower=False, transpose_a=True)
    update = lax.linalg.triangular_solve(factor, coupling, left_side=True, lower=False, transpose_a=False)
    update = update.astype(jnp.bfloat16)
    remainder = (wide_slab - jnp.dot(panel.astype(jnp.float32), update.astype(jnp.float32), preferred_element_type=jnp.float32)).astype(jnp.bfloat16)
    return (factor, coupling, remainder)
```

```python
import jax
import jax.numpy as jnp
from jax import lax
from jax.experimental import pallas as pl
from jax.experimental.pallas import tpu as pltpu

HI = lax.Precision.HIGHEST


def mm(a, b, ca=1, cb=0):
    return lax.dot_general(a, b, (((ca,), (cb,)), ((), ())), precision=HI, preferred_element_type=jnp.float32)


def eliminate(block, r_ref, w_ref):
    n = block.shape[0]
    groups = n // 8
    lane = lax.broadcasted_iota(jnp.int32, (8, n), 1)
    sub = lax.broadcasted_iota(jnp.int32, (8, n), 0)
    a = [block[8 * t : 8 * t + 8, :] for t in range(groups)]
    w = [jnp.where(lane == sub + 8 * t, 1.0, 0.0).astype(jnp.float32) for t in range(groups)]

    def group(g, carry):
        a, w = list(carry[0]), list(carry[1])
        for j in range(8):
            inv = lax.rsqrt(jnp.broadcast_to(a[0][j : j + 1, j : j + 1], (8, n)))
            arow = jnp.broadcast_to(a[0][j : j + 1, :], (8, n)) * inv
            wrow = jnp.broadcast_to(w[0][j : j + 1, :], (8, n)) * inv
            for t in range(groups):
                col = jnp.broadcast_to(a[t][:, j : j + 1], (8, n)) * inv
                if t == 0:
                    below = sub > j
                    here = sub == j
                    a[0], w[0] = (
                        jnp.where(here, arow, jnp.where(below, a[0] - col * arow, a[0])),
                        jnp.where(here, wrow, jnp.where(below, w[0] - col * wrow, w[0])),
                    )
                else:
                    a[t] = a[t] - col * arow
                    w[t] = w[t] - col * wrow
        start = pl.multiple_of(8 * g, 8)
        r = pltpu.roll(a[0], 8 * g, 1)
        r_ref[pl.ds(start, 8), :] = jnp.where(lane >= sub + 8 * g, r, 0.0)
        w_ref[pl.ds(start, 8), :] = w[0]
        zero = jnp.zeros((8, n), jnp.float32)
        a = [pltpu.roll(x, n - 8, 1) for x in a[1:]] + [zero]
        w = w[1:] + [zero]
        return tuple(a), tuple(w)

    lax.fori_loop(0, groups, group, (tuple(a), tuple(w)))


def factor_kernel(gram_ref, factor_ref, invt_ref, r_ref, w_ref):
    h = gram_ref.shape[0] // 2
    eliminate(gram_ref[:h, :h], r_ref, w_ref)
    w1 = w_ref[...]
    factor_ref[:h, :h] = r_ref[...]
    invt_ref[:h, :h] = w1
    r12 = mm(w1, gram_ref[:h, h:])
    factor_ref[:h, h:] = r12
    factor_ref[h:, :h] = jnp.zeros((h, h), jnp.float32)
    invt_ref[:h, h:] = jnp.zeros((h, h), jnp.float32)
    eliminate(gram_ref[h:, h:] - mm(r12, r12, 0, 0), r_ref, w_ref)
    w2 = w_ref[...]
    factor_ref[h:, h:] = r_ref[...]
    invt_ref[h:, h:] = w2
    invt_ref[h:, :h] = -mm(w2, mm(r12, w1, 0, 0))


def factor_and_invt(gram):
    n = gram.shape[0]
    h = n // 2
    out = jax.ShapeDtypeStruct((n, n), jnp.float32)
    return pl.pallas_call(
        factor_kernel,
        out_shape=(out, out),
        scratch_shapes=[pltpu.VMEM((h, h), jnp.float32), pltpu.VMEM((h, h), jnp.float32)],
        cost_estimate=pl.CostEstimate(flops=60_000_000, bytes_accessed=3 * n * n * 4, transcendentals=n),
        name="factor",
    )(gram)


def on_device(panel, slab):
    total_rows = panel.shape[0] * lax.axis_size("row")
    scale = 1.0 / total_rows
    contract = (((0,), (0,)), ((), ()))
    gram = lax.psum(lax.dot_general(panel, panel, contract, preferred_element_type=jnp.float32) * scale, "row")
    local_cross = lax.dot_general(panel, slab, contract, preferred_element_type=jnp.float32) * scale
    cross = lax.psum(local_cross, "row")
    factor, invt = factor_and_invt(gram)
    coupling = mm(invt, cross)
    update = mm(invt, coupling, 0, 0).astype(jnp.bfloat16)
    remainder = (slab.astype(jnp.float32) - jnp.dot(panel, update, preferred_element_type=jnp.float32)).astype(jnp.bfloat16)
    share = factor.shape[1] // lax.axis_size("col")
    factor_part = lax.dynamic_slice_in_dim(factor, lax.axis_index("col") * share, share, 1)
    return (factor_part, coupling, remainder)


def solution(mesh):
    from jax.sharding import PartitionSpec as P

    return jax.shard_map(
        on_device,
        mesh=mesh,
        in_specs=(P("row", None), P("row", "col")),
        out_specs=(P(None, "col"), P(None, "col"), P("row", "col")),
        check_vma=False,
    )
```

```python
import functools

import jax
import jax.numpy as jnp
from jax import lax
from jax.experimental import pallas as pl
from jax.experimental.pallas import tpu as pltpu
from jax.sharding import PartitionSpec as P

HI = lax.Precision.HIGHEST


def mm(a, b, ca=1, cb=0):
    return lax.dot_general(a, b, (((ca,), (cb,)), ((), ())), precision=HI, preferred_element_type=jnp.float32)


def eliminate(block, r_ref, w_ref):
    n = block.shape[0]
    groups = n // 8
    lane = lax.broadcasted_iota(jnp.int32, (8, n), 1)
    sub = lax.broadcasted_iota(jnp.int32, (8, n), 0)
    a = [block[8 * t : 8 * t + 8, :] for t in range(groups)]
    w = [jnp.where(lane == sub + 8 * t, 1.0, 0.0).astype(jnp.float32) for t in range(groups)]

    def group(g, carry):
        a, w = list(carry[0]), list(carry[1])
        for j in range(8):
            inv = lax.rsqrt(jnp.broadcast_to(a[0][j : j + 1, j : j + 1], (8, n)))
            arow = jnp.broadcast_to(a[0][j : j + 1, :], (8, n)) * inv
            wrow = jnp.broadcast_to(w[0][j : j + 1, :], (8, n)) * inv
            for t in range(groups):
                col = jnp.broadcast_to(a[t][:, j : j + 1], (8, n)) * inv
                if t == 0:
                    below = sub > j
                    here = sub == j
                    a[0], w[0] = (
                        jnp.where(here, arow, jnp.where(below, a[0] - col * arow, a[0])),
                        jnp.where(here, wrow, jnp.where(below, w[0] - col * wrow, w[0])),
                    )
                else:
                    a[t] = a[t] - col * arow
                    w[t] = w[t] - col * wrow
        start = pl.multiple_of(8 * g, 8)
        r = pltpu.roll(a[0], 8 * g, 1)
        r_ref[pl.ds(start, 8), :] = jnp.where(lane >= sub + 8 * g, r, 0.0)
        w_ref[pl.ds(start, 8), :] = w[0]
        zero = jnp.zeros((8, n), jnp.float32)
        a = [pltpu.roll(x, n - 8, 1) for x in a[1:]] + [zero]
        w = w[1:] + [zero]
        return tuple(a), tuple(w)

    lax.fori_loop(0, groups, group, (tuple(a), tuple(w)))


def fused_kernel(
    n, ncol, gram_ref, cross_ref, factor_ref, invt_ref, full_ref,
    gbuf, cbuf, gfull, cfull, gown, cown, r_ref, w_ref,
    gs_send, gs_recv, ga_send, ga_recv, fw_send, fw_recv, cs_send, cs_recv, ca_send, ca_recv,
):
    me, mc = lax.axis_index("row"), lax.axis_index("col")
    order = gram_ref.shape[1]
    part = gram_ref.shape[0]
    gchunk, cchunk = gown.shape[0], cown.shape[0]
    gowners, cowners = part // gchunk, order // cchunk

    def peers(body):
        def step(k, _):
            body(lax.rem(me + k, n))
            return 0

        lax.fori_loop(1, n, step, 0)

    def cols(body):
        def step(k, _):
            body(lax.rem(mc + k, ncol))
            return 0

        lax.fori_loop(1, ncol, step, 0)

    def owned(owners, who, body):
        if owners == n:
            body()
        else:
            pl.when(who < owners)(body)

    def remote(src, dst, send, recv, row, col):
        return pltpu.make_async_remote_copy(
            src_ref=src, dst_ref=dst, send_sem=send, recv_sem=recv,
            device_id={"row": row, "col": col}, device_id_type=pl.DeviceIdType.MESH,
        )

    barrier = pltpu.get_barrier_semaphore()
    peers(lambda p: pl.semaphore_signal(barrier, inc=1, device_id={"row": p, "col": mc}, device_id_type=pl.DeviceIdType.MESH))
    cols(lambda q: pl.semaphore_signal(barrier, inc=1, device_id={"row": me, "col": q}, device_id_type=pl.DeviceIdType.MESH))
    pl.semaphore_wait(barrier, n + ncol - 2)

    def rows(owner, chunk):
        return pl.ds(pl.multiple_of(owner * chunk, 8), chunk)

    def grows(owner, col):
        return pl.ds(pl.multiple_of(col * part + owner * gchunk, 8), gchunk)

    def gs(src, dst):
        return remote(gram_ref.at[rows(dst, gchunk)], gbuf.at[src], gs_send.at[dst], gs_recv.at[src], dst, mc)

    def ga(owner, dst):
        return remote(gown, gfull.at[grows(owner, mc)], ga_send.at[dst], ga_recv.at[owner], dst, mc)

    def fw(owner, col, dst):
        return remote(
            gfull.at[grows(owner, col)], gfull.at[grows(owner, col)],
            fw_send.at[owner, dst], fw_recv.at[owner, col], me, dst,
        )

    def cs(src, dst):
        return remote(cross_ref.at[rows(dst, cchunk)], cbuf.at[src], cs_send.at[dst], cs_recv.at[src], dst, mc)

    def ca(owner, dst):
        return remote(cown, cfull.at[rows(owner, cchunk)], ca_send.at[dst], ca_recv.at[owner], dst, mc)

    peers(lambda p: owned(gowners, p, lambda: gs(me, p).start()))

    def sum_gram():
        gown[...] = gram_ref[rows(me, gchunk), :]

        def add(p):
            gs(p, me).wait_recv()
            gown[...] += gbuf[p]

        peers(add)
        gfull[grows(me, mc), :] = gown[...]
        peers(lambda p: ga(me, p).start())
        cols(lambda q: remote(
            gown, gfull.at[grows(me, mc)], fw_send.at[me, q], fw_recv.at[me, mc], me, q).start())

    owned(gowners, me, sum_gram)
    peers(lambda p: owned(cowners, p, lambda: cs(me, p).start()))

    def relay(p):
        def go():
            ga(p, me).wait_recv()
            cols(lambda q: fw(p, mc, q).start())

        owned(gowners, p, go)

    peers(relay)

    def relayed(q):
        def each(o, _):
            fw(o, q, mc).wait_recv()
            return 0

        lax.fori_loop(0, gowners, each, 0)

    cols(relayed)

    h = order // 2
    eliminate(gfull[:h, :h], r_ref, w_ref)
    w1 = w_ref[...]
    factor_ref[:h, :h] = r_ref[...]
    invt_ref[:h, :h] = w1
    r12 = mm(w1, gfull[:h, h:])
    factor_ref[:h, h:] = r12
    factor_ref[h:, :h] = jnp.zeros((h, h), jnp.float32)
    invt_ref[:h, h:] = jnp.zeros((h, h), jnp.float32)
    lower = gfull[h:, h:] - mm(r12, r12, 0, 0)

    def sum_cross():
        cown[...] = cross_ref[rows(me, cchunk), :]

        def add(p):
            cs(p, me).wait_recv()
            cown[...] += cbuf[p]

        peers(add)
        cfull[rows(me, cchunk), :] = cown[...]
        peers(lambda p: ca(me, p).start())

    owned(cowners, me, sum_cross)

    eliminate(lower, r_ref, w_ref)
    w2 = w_ref[...]
    factor_ref[h:, h:] = r_ref[...]
    invt_ref[h:, h:] = w2
    invt_ref[h:, :h] = -mm(w2, mm(r12, w1, 0, 0))

    peers(lambda p: owned(cowners, p, lambda: ca(p, me).wait_recv()))
    full_ref[...] = cfull[...]
    peers(lambda p: owned(gowners, p, lambda: gs(me, p).wait_send()))
    peers(lambda p: owned(cowners, p, lambda: cs(me, p).wait_send()))
    owned(gowners, me, lambda: peers(lambda p: ga(me, p).wait_send()))
    owned(cowners, me, lambda: peers(lambda p: ca(me, p).wait_send()))

    def sent(q):
        def each(o, _):
            fw(o, mc, q).wait_send()
            return 0

        lax.fori_loop(0, gowners, each, 0)

    cols(sent)


def sums_and_factor(gram, cross, n, ncol):
    part, order = gram.shape
    width = cross.shape[1]
    gchunk = max(8, part // n)
    cchunk = max(8, order // n)
    f32 = jnp.float32
    dma = pltpu.SemaphoreType.DMA
    square = jax.ShapeDtypeStruct((order, order), f32)
    h = order // 2
    return pl.pallas_call(
        functools.partial(fused_kernel, n, ncol),
        out_shape=(square, square, jax.ShapeDtypeStruct((order, width), f32)),
        in_specs=[pl.BlockSpec(memory_space=pltpu.VMEM)] * 2,
        out_specs=[pl.BlockSpec(memory_space=pltpu.VMEM)] * 3,
        scratch_shapes=[
            pltpu.VMEM((n, gchunk, order), f32),
            pltpu.VMEM((n, cchunk, width), f32),
            pltpu.VMEM((order, order), f32),
            pltpu.VMEM((order, width), f32),
            pltpu.VMEM((gchunk, order), f32),
            pltpu.VMEM((cchunk, width), f32),
            pltpu.VMEM((h, h), f32),
            pltpu.VMEM((h, h), f32),
            dma((n,)), dma((n,)), dma((n,)), dma((n,)),
            dma((n, ncol)), dma((n, ncol)),
            dma((n,)), dma((n,)), dma((n,)), dma((n,)),
        ],
        compiler_params=pltpu.CompilerParams(collective_id=0, has_side_effects=True),
        name="sums_and_factor",
    )(gram, cross)


def finish_kernel(factor_ref, invt_ref, cross_ref, panel_ref, slab_ref, part_ref, coupling_ref, out_ref, update):
    @pl.when(pl.program_id(0) == 0)
    def _():
        share = part_ref.shape[1]
        for q in range(factor_ref.shape[1] // share):

            @pl.when(lax.axis_index("col") == q)
            def _(q=q):
                part_ref[...] = factor_ref[:, q * share : (q + 1) * share]

        invt = invt_ref[...]
        coupling = mm(invt, cross_ref[...])
        coupling_ref[...] = coupling
        update[...] = mm(invt, coupling, 0, 0).astype(jnp.bfloat16)

    product = jnp.dot(panel_ref[...], update[...], preferred_element_type=jnp.float32)
    out_ref[...] = (slab_ref[...].astype(jnp.float32) - product).astype(jnp.bfloat16)


def finish(factor, invt, cross, panel, slab, ncol):
    order, width = cross.shape
    height = panel.shape[0]
    tile = max(height // 8, 8)
    share = order // ncol
    whole = lambda shape: pl.BlockSpec(shape, lambda i: (0, 0))
    return pl.pallas_call(
        finish_kernel,
        grid=(height // tile,),
        out_shape=(
            jax.ShapeDtypeStruct((order, share), jnp.float32),
            jax.ShapeDtypeStruct((order, width), jnp.float32),
            jax.ShapeDtypeStruct((height, width), jnp.bfloat16),
        ),
        in_specs=[
            whole((order, order)), whole((order, order)), whole((order, width)),
            pl.BlockSpec((tile, order), lambda i: (i, 0)),
            pl.BlockSpec((tile, width), lambda i: (i, 0)),
        ],
        out_specs=(whole((order, share)), whole((order, width)), pl.BlockSpec((tile, width), lambda i: (i, 0))),
        scratch_shapes=[pltpu.VMEM((order, width), jnp.bfloat16)],
        name="finish",
    )(factor, invt, cross, panel, slab)


def on_device(panel, slab):
    n, ncol = lax.axis_size("row"), lax.axis_size("col")
    scale = 1.0 / (panel.shape[0] * n)
    contract = (((0,), (0,)), ((), ()))
    part = panel.shape[1] // ncol
    mine = lax.dynamic_slice_in_dim(panel, lax.axis_index("col") * part, part, 1)
    gram = lax.dot_general(mine, panel, contract, preferred_element_type=jnp.float32) * scale
    cross = lax.dot_general(panel, slab, contract, preferred_element_type=jnp.float32) * scale
    factor, invt, cross = sums_and_factor(gram, cross, n, ncol)
    return finish(factor, invt, cross, panel, slab, ncol)


def solution(mesh):
    return jax.shard_map(
        on_device,
        mesh=mesh,
        in_specs=(P("row", None), P("row", "col")),
        out_specs=(P(None, "col"), P(None, "col"), P("row", "col")),
        check_vma=False,
    )
```

```python
import functools

import jax
import jax.numpy as jnp
from jax import lax
from jax.experimental import pallas as pl
from jax.experimental.pallas import tpu as pltpu
from jax.sharding import PartitionSpec as P

HI = lax.Precision.HIGHEST


def mm(a, b, ca=1, cb=0):
    return lax.dot_general(a, b, (((ca,), (cb,)), ((), ())), precision=HI, preferred_element_type=jnp.float32)


def eliminate(block, r_ref, w_ref):
    n = block.shape[0]
    groups = n // 8
    lane = lax.broadcasted_iota(jnp.int32, (8, n), 1)
    sub = lax.broadcasted_iota(jnp.int32, (8, n), 0)
    a = [block[8 * t : 8 * t + 8, :] for t in range(groups)]
    w = [jnp.where(lane == sub + 8 * t, 1.0, 0.0).astype(jnp.float32) for t in range(groups)]

    def group(g, carry):
        a, w = list(carry[0]), list(carry[1])
        top, wtop = a[0], w[0]
        cols = [jnp.broadcast_to(top[:, j : j + 1], (8, n)) for j in range(8)]
        scale = jnp.zeros((8, n), jnp.float32)
        for j in range(8):
            inv = lax.rsqrt(jnp.broadcast_to(cols[j][j : j + 1, :], (8, n)))
            scale = jnp.where(sub == j, inv, scale)
            m = jnp.where(sub > j, cols[j], 0.0) * inv * inv
            for i in range(j + 1, 8):
                cols[i] = cols[i] - m * jnp.broadcast_to(cols[i][j : j + 1, :], (8, n))
            top = top - m * jnp.broadcast_to(top[j : j + 1, :], (8, n))
            wtop = wtop - m * jnp.broadcast_to(wtop[j : j + 1, :], (8, n))
        top, wtop = top * scale, wtop * scale
        start = pl.multiple_of(8 * g, 8)
        r_ref[pl.ds(start, 8), :] = jnp.where(lane >= sub + 8 * g, pltpu.roll(top, 8 * g, 1), 0.0)
        w_ref[pl.ds(start, 8), :] = wtop
        u = mm(top, jnp.concatenate([top, wtop], axis=1), 0, 0)
        zero = jnp.zeros((8, n), jnp.float32)
        a = [pltpu.roll(a[t] - u[8 * t : 8 * t + 8, :n], n - 8, 1) for t in range(1, groups)] + [zero]
        w = [w[t] - u[8 * t : 8 * t + 8, n:] for t in range(1, groups)] + [zero]
        return tuple(a), tuple(w)

    lax.fori_loop(0, groups, group, (tuple(a), tuple(w)))


def fused_kernel(
    n, ncol, scale, panel_hbm, slab_hbm, factor_ref, invt_ref, full_ref,
    panel_ref, slab_ref, panel_sem, slab_sem, gram_ref, cross_ref, gbuf, cbuf, gfull, cfull, gown, cown, r_ref, w_ref,
    gs_send, gs_recv, ga_send, ga_recv, fw_send, fw_recv, cs_send, cs_recv, ca_send, ca_recv,
):
    me, mc = lax.axis_index("row"), lax.axis_index("col")
    get_panel = pltpu.make_async_copy(panel_hbm, panel_ref, panel_sem)
    get_panel.start()
    get_slab = pltpu.make_async_copy(slab_hbm, slab_ref, slab_sem)
    get_slab.start()
    order = gram_ref.shape[1]
    part = gram_ref.shape[0]
    gchunk, cchunk = gown.shape[0], cown.shape[0]
    gowners, cowners = part // gchunk, order // cchunk

    def peers(body):
        def step(k, _):
            body(lax.rem(me + k, n))
            return 0

        lax.fori_loop(1, n, step, 0)

    def sources(body):
        def step(k, _):
            body(lax.rem(me + n - k, n))
            return 0

        lax.fori_loop(1, n, step, 0)

    def cols(body):
        def step(k, _):
            body(lax.rem(mc + k, ncol))
            return 0

        lax.fori_loop(1, ncol, step, 0)

    def owned(owners, who, body):
        if owners == n:
            body()
        else:
            pl.when(who < owners)(body)

    def remote(src, dst, send, recv, row, col):
        return pltpu.make_async_remote_copy(
            src_ref=src, dst_ref=dst, send_sem=send, recv_sem=recv,
            device_id={"row": row, "col": col}, device_id_type=pl.DeviceIdType.MESH,
        )

    barrier = pltpu.get_barrier_semaphore()
    peers(lambda p: pl.semaphore_signal(barrier, inc=1, device_id={"row": p, "col": mc}, device_id_type=pl.DeviceIdType.MESH))
    cols(lambda q: pl.semaphore_signal(barrier, inc=1, device_id={"row": me, "col": q}, device_id_type=pl.DeviceIdType.MESH))
    height = panel_ref.shape[0]
    tile = height // 4
    contract = (((0,), (0,)), ((), ()))
    get_panel.wait()
    for q in range(ncol):

        @pl.when(mc == q)
        def _(q=q):
            gram_ref[...] = jnp.zeros_like(gram_ref)

            def gram_step(t, _):
                at = pl.ds(pl.multiple_of(t * tile, tile), tile)
                gram_ref[...] += lax.dot_general(
                    panel_ref[at, q * part : (q + 1) * part], panel_ref[at, :], contract, preferred_element_type=jnp.float32
                )
                return 0

            lax.fori_loop(0, height // tile, gram_step, 0)

    gram_ref[...] *= scale
    pl.semaphore_wait(barrier, n + ncol - 2)

    def rows(owner, chunk):
        return pl.ds(pl.multiple_of(owner * chunk, 8), chunk)

    def grows(owner, col):
        return pl.ds(pl.multiple_of(col * part + owner * gchunk, 8), gchunk)

    def gs(src, dst):
        return remote(gram_ref.at[rows(dst, gchunk)], gbuf.at[src], gs_send.at[dst], gs_recv.at[src], dst, mc)

    def ga(owner, dst):
        return remote(gown, gfull.at[grows(owner, mc)], ga_send.at[dst], ga_recv.at[owner], dst, mc)

    def fw(owner, col, dst):
        return remote(
            gfull.at[grows(owner, col)], gfull.at[grows(owner, col)],
            fw_send.at[owner, dst], fw_recv.at[owner, col], me, dst,
        )

    def cs(src, dst):
        return remote(cross_ref.at[rows(dst, cchunk)], cbuf.at[src], cs_send.at[dst], cs_recv.at[src], dst, mc)

    def ca(owner, dst):
        return remote(cown, cfull.at[rows(owner, cchunk)], ca_send.at[dst], ca_recv.at[owner], dst, mc)

    peers(lambda p: owned(gowners, p, lambda: gs(me, p).start()))

    get_slab.wait()
    cross_ref[...] = jnp.zeros_like(cross_ref)

    def cross_step(t, _):
        at = pl.ds(pl.multiple_of(t * tile, tile), tile)
        cross_ref[...] += lax.dot_general(panel_ref[at, :], slab_ref[at, :], contract, preferred_element_type=jnp.float32)
        return 0

    lax.fori_loop(0, height // tile, cross_step, 0)
    cross_ref[...] *= scale

    def sum_gram():
        gown[...] = gram_ref[rows(me, gchunk), :]

        def add(p):
            gs(p, me).wait_recv()
            gown[...] += gbuf[p]

        sources(add)
        gfull[grows(me, mc), :] = gown[...]
        peers(lambda p: ga(me, p).start())
        cols(lambda q: remote(
            gown, gfull.at[grows(me, mc)], fw_send.at[me, q], fw_recv.at[me, mc], me, q).start())

    owned(gowners, me, sum_gram)
    peers(lambda p: owned(cowners, p, lambda: cs(me, p).start()))

    def relay(p):
        def go():
            ga(p, me).wait_recv()
            cols(lambda q: fw(p, mc, q).start())

        owned(gowners, p, go)

    sources(relay)

    def relayed(q):
        def each(o, _):
            fw(o, q, mc).wait_recv()
            return 0

        lax.fori_loop(0, gowners, each, 0)

    cols(relayed)

    h = order // 2
    eliminate(gfull[:h, :h], r_ref, w_ref)
    w1 = w_ref[...]
    factor_ref[:h, :h] = r_ref[...]
    invt_ref[:h, :h] = w1
    r12 = mm(w1, gfull[:h, h:])
    factor_ref[:h, h:] = r12
    factor_ref[h:, :h] = jnp.zeros((h, h), jnp.float32)
    invt_ref[:h, h:] = jnp.zeros((h, h), jnp.float32)
    lower = gfull[h:, h:] - mm(r12, r12, 0, 0)

    def sum_cross():
        cown[...] = cross_ref[rows(me, cchunk), :]

        def add(p):
            cs(p, me).wait_recv()
            cown[...] += cbuf[p]

        sources(add)
        cfull[rows(me, cchunk), :] = cown[...]
        peers(lambda p: ca(me, p).start())

    owned(cowners, me, sum_cross)

    eliminate(lower, r_ref, w_ref)
    w2 = w_ref[...]
    factor_ref[h:, h:] = r_ref[...]
    invt_ref[h:, h:] = w2
    invt_ref[h:, :h] = -mm(w2, mm(r12, w1, 0, 0))

    peers(lambda p: owned(cowners, p, lambda: ca(p, me).wait_recv()))
    full_ref[...] = cfull[...]
    peers(lambda p: owned(gowners, p, lambda: gs(me, p).wait_send()))
    peers(lambda p: owned(cowners, p, lambda: cs(me, p).wait_send()))
    owned(gowners, me, lambda: peers(lambda p: ga(me, p).wait_send()))
    owned(cowners, me, lambda: peers(lambda p: ca(me, p).wait_send()))

    def sent(q):
        def each(o, _):
            fw(o, mc, q).wait_send()
            return 0

        lax.fori_loop(0, gowners, each, 0)

    cols(sent)


def sums_and_factor(panel, slab, n, ncol):
    height, order = panel.shape
    width = slab.shape[1]
    part = order // ncol
    scale = 1.0 / (height * n)
    gchunk = max(8, part // n)
    cchunk = max(8, order // n)
    f32 = jnp.float32
    dma = pltpu.SemaphoreType.DMA
    square = jax.ShapeDtypeStruct((order, order), f32)
    h = order // 2
    return pl.pallas_call(
        functools.partial(fused_kernel, n, ncol, scale),
        out_shape=(square, square, jax.ShapeDtypeStruct((order, width), f32)),
        in_specs=[pl.BlockSpec(memory_space=pl.ANY)] * 2,
        out_specs=[pl.BlockSpec(memory_space=pltpu.VMEM)] * 3,
        scratch_shapes=[
            pltpu.VMEM(panel.shape, panel.dtype),
            pltpu.VMEM(slab.shape, slab.dtype),
            dma, dma,
            pltpu.VMEM((part, order), f32),
            pltpu.VMEM((order, width), f32),
            pltpu.VMEM((n, gchunk, order), f32),
            pltpu.VMEM((n, cchunk, width), f32),
            pltpu.VMEM((order, order), f32),
            pltpu.VMEM((order, width), f32),
            pltpu.VMEM((gchunk, order), f32),
            pltpu.VMEM((cchunk, width), f32),
            pltpu.VMEM((h, h), f32),
            pltpu.VMEM((h, h), f32),
            dma((n,)), dma((n,)), dma((n,)), dma((n,)),
            dma((n, ncol)), dma((n, ncol)),
            dma((n,)), dma((n,)), dma((n,)), dma((n,)),
        ],
        compiler_params=pltpu.CompilerParams(collective_id=0, has_side_effects=True),
        name="sums_and_factor",
    )(panel, slab)


def finish_kernel(
    tiles, factor_ref, invt_ref, cross_ref, panel_hbm, slab_hbm, part_ref, coupling_hbm, out_hbm,
    panel_ref, slab_ref, out_ref, coupling_ref, panel_sem, slab_sem, out_sem, coupling_sem,
):
    tile = panel_ref.shape[0] // tiles
    rows = [pl.ds(t * tile, tile) for t in range(tiles)]
    get_panel = [pltpu.make_async_copy(panel_hbm.at[rows[t]], panel_ref.at[rows[t]], panel_sem.at[t]) for t in range(tiles)]
    get_slab = [pltpu.make_async_copy(slab_hbm.at[rows[t]], slab_ref.at[rows[t]], slab_sem.at[t]) for t in range(tiles)]
    put_out = [pltpu.make_async_copy(out_ref.at[rows[t]], out_hbm.at[rows[t]], out_sem.at[t]) for t in range(tiles)]
    put_coupling = pltpu.make_async_copy(coupling_ref, coupling_hbm, coupling_sem)
    for t in range(tiles):
        get_panel[t].start()
        get_slab[t].start()
    share = part_ref.shape[1]
    for q in range(factor_ref.shape[1] // share):

        @pl.when(lax.axis_index("col") == q)
        def _(q=q):
            part_ref[...] = factor_ref[:, q * share : (q + 1) * share]

    invt = invt_ref[...]
    coupling = mm(invt, cross_ref[...])
    coupling_ref[...] = coupling
    put_coupling.start()
    update = mm(invt, coupling, 0, 0).astype(jnp.bfloat16)
    for t in range(tiles):
        get_panel[t].wait()
        get_slab[t].wait()
        product = jnp.dot(panel_ref[rows[t], :], update, preferred_element_type=jnp.float32)
        out_ref[rows[t], :] = (slab_ref[rows[t], :].astype(jnp.float32) - product).astype(jnp.bfloat16)
        put_out[t].start()
    for t in range(tiles):
        put_out[t].wait()
    put_coupling.wait()


def finish(factor, invt, cross, panel, slab, ncol):
    order, width = cross.shape
    tiles = 8
    vmem, hbm = pl.BlockSpec(memory_space=pltpu.VMEM), pl.BlockSpec(memory_space=pl.ANY)
    dma = pltpu.SemaphoreType.DMA
    return pl.pallas_call(
        functools.partial(finish_kernel, tiles),
        out_shape=(
            jax.ShapeDtypeStruct((order, order // ncol), jnp.float32),
            jax.ShapeDtypeStruct((order, width), jnp.float32),
            jax.ShapeDtypeStruct(slab.shape, slab.dtype),
        ),
        in_specs=[vmem, vmem, vmem, hbm, hbm],
        out_specs=(vmem, hbm, hbm),
        scratch_shapes=[
            pltpu.VMEM(panel.shape, panel.dtype),
            pltpu.VMEM(slab.shape, slab.dtype),
            pltpu.VMEM(slab.shape, slab.dtype),
            pltpu.VMEM((order, width), jnp.float32),
            dma((tiles,)), dma((tiles,)), dma((tiles,)), dma,
        ],
        name="finish",
    )(factor, invt, cross, panel, slab)


def on_device(panel, slab):
    n, ncol = lax.axis_size("row"), lax.axis_size("col")
    factor, invt, cross = sums_and_factor(panel, slab, n, ncol)
    return finish(factor, invt, cross, panel, slab, ncol)


def solution(mesh):
    return jax.shard_map(
        on_device,
        mesh=mesh,
        in_specs=(P("row", None), P("row", "col")),
        out_specs=(P(None, "col"), P(None, "col"), P("row", "col")),
        check_vma=False,
    )
```

```python
import functools

import jax
import jax.numpy as jnp
from jax import lax
from jax.experimental import pallas as pl
from jax.experimental.pallas import tpu as pltpu
from jax.sharding import PartitionSpec as P

HI = lax.Precision.HIGHEST


def mm(a, b, ca=1, cb=0):
    return lax.dot_general(a, b, (((ca,), (cb,)), ((), ())), precision=HI, preferred_element_type=jnp.float32)


def eliminate(block, r_ref, w_ref, midway):
    n = block.shape[0]
    groups = n // 8
    lane = lax.broadcasted_iota(jnp.int32, (8, n), 1)
    sub = lax.broadcasted_iota(jnp.int32, (8, n), 0)
    a = [block[8 * t : 8 * t + 8, :] for t in range(groups)]
    w = [jnp.where(lane == sub + 8 * t, 1.0, 0.0).astype(jnp.float32) for t in range(groups)]

    def group(g, carry):
        a, w = list(carry[0]), list(carry[1])
        top, wtop = a[0], w[0]
        cols = [jnp.broadcast_to(top[:, j : j + 1], (8, n)) for j in range(8)]
        scale = jnp.zeros((8, n), jnp.float32)
        for j in range(8):
            inv = lax.rsqrt(jnp.broadcast_to(cols[j][j : j + 1, :], (8, n)))
            scale = jnp.where(sub == j, inv, scale)
            m = jnp.where(sub > j, cols[j], 0.0) * inv * inv
            for i in range(j + 1, 8):
                cols[i] = cols[i] - m * jnp.broadcast_to(cols[i][j : j + 1, :], (8, n))
            top = top - m * jnp.broadcast_to(top[j : j + 1, :], (8, n))
            wtop = wtop - m * jnp.broadcast_to(wtop[j : j + 1, :], (8, n))
        top, wtop = top * scale, wtop * scale
        start = pl.multiple_of(8 * g, 8)
        r_ref[pl.ds(start, 8), :] = jnp.where(lane >= sub + 8 * g, pltpu.roll(top, 8 * g, 1), 0.0)
        w_ref[pl.ds(start, 8), :] = wtop
        u = mm(top, jnp.concatenate([top, wtop], axis=1), 0, 0)
        zero = jnp.zeros((8, n), jnp.float32)
        a = [pltpu.roll(a[t] - u[8 * t : 8 * t + 8, :n], n - 8, 1) for t in range(1, groups)] + [zero]
        w = [w[t] - u[8 * t : 8 * t + 8, n:] for t in range(1, groups)] + [zero]
        return tuple(a), tuple(w)

    carry = lax.fori_loop(0, groups // 2, group, (tuple(a), tuple(w)))
    midway()
    lax.fori_loop(groups // 2, groups, group, carry)


def fused_kernel(
    n, ni, ncol, scale, panel_hbm, slab_hbm, factor_ref, invt_ref, full_ref,
    panel_ref, slab_ref, panel_sem, slab_sem, gram_ref, cross_ref, gbuf, cbuf, partial, outer_buf, gfull, cfull, gown, cown, r_ref, w_ref,
    gs_send, gs_recv, ga_send, ga_recv, fw_send, fw_recv, c1_send, c1_recv, c2_send, c2_recv, ca_send, ca_recv, cf_send, cf_recv,
):
    me, mc = lax.axis_index("row"), lax.axis_index("col")
    get_panel = pltpu.make_async_copy(panel_hbm, panel_ref, panel_sem)
    get_panel.start()
    get_slab = pltpu.make_async_copy(slab_hbm, slab_ref, slab_sem)
    get_slab.start()
    order = gram_ref.shape[1]
    part = gram_ref.shape[0]
    gchunk, cchunk = gown.shape[0], cown.shape[0]
    gowners, cowners = part // gchunk, order // ni // cchunk
    no = n // ni
    mo, mi = me // ni, lax.rem(me, ni)

    def outer(body):
        def step(k, _):
            body(lax.rem(mo + k, no))
            return 0

        lax.fori_loop(1, no, step, 0)

    def inner(body):
        def step(k, _):
            body(lax.rem(mi + k, ni))
            return 0

        lax.fori_loop(1, ni, step, 0)

    def pieces(body):
        def step(k, _):
            body(lax.rem(mo + 1 + k, cowners))
            return 0

        lax.fori_loop(0, cowners, step, 0)

    def peers(body):
        def step(k, _):
            body(lax.rem(me + k, n))
            return 0

        lax.fori_loop(1, n, step, 0)

    def sources(body):
        def step(k, _):
            body(lax.rem(me + n - k, n))
            return 0

        lax.fori_loop(1, n, step, 0)

    def cols(body):
        def step(k, _):
            body(lax.rem(mc + k, ncol))
            return 0

        lax.fori_loop(1, ncol, step, 0)

    def owned(owners, who, body):
        if owners == n:
            body()
        else:
            pl.when(who < owners)(body)

    def remote(src, dst, send, recv, row, col):
        return pltpu.make_async_remote_copy(
            src_ref=src, dst_ref=dst, send_sem=send, recv_sem=recv,
            device_id={"row": row, "col": col}, device_id_type=pl.DeviceIdType.MESH,
        )

    barrier = pltpu.get_barrier_semaphore()
    peers(lambda p: pl.semaphore_signal(barrier, inc=1, device_id={"row": p, "col": mc}, device_id_type=pl.DeviceIdType.MESH))
    cols(lambda q: pl.semaphore_signal(barrier, inc=1, device_id={"row": me, "col": q}, device_id_type=pl.DeviceIdType.MESH))
    height = panel_ref.shape[0]
    tile = height // 4
    contract = (((0,), (0,)), ((), ()))
    get_panel.wait()
    for q in range(ncol):

        @pl.when(mc == q)
        def _(q=q):
            gram_ref[...] = jnp.zeros_like(gram_ref)

            def gram_step(t, _):
                at = pl.ds(pl.multiple_of(t * tile, tile), tile)
                gram_ref[...] += lax.dot_general(
                    panel_ref[at, q * part : (q + 1) * part], panel_ref[at, :], contract, preferred_element_type=jnp.float32
                )
                return 0

            lax.fori_loop(0, height // tile, gram_step, 0)

    gram_ref[...] *= scale
    pl.semaphore_wait(barrier, n + ncol - 2)

    def rows(owner, chunk):
        return pl.ds(pl.multiple_of(owner * chunk, 8), chunk)

    def grows(owner, col):
        return pl.ds(pl.multiple_of(col * part + owner * gchunk, 8), gchunk)

    def gs(src, dst):
        return remote(gram_ref.at[rows(dst, gchunk)], gbuf.at[src], gs_send.at[dst], gs_recv.at[src], dst, mc)

    def ga(owner, dst):
        return remote(gown, gfull.at[grows(owner, mc)], ga_send.at[dst], ga_recv.at[owner], dst, mc)

    def fw(owner, col, dst):
        return remote(
            gfull.at[grows(owner, col)], gfull.at[grows(owner, col)],
            fw_send.at[owner, dst], fw_recv.at[owner, col], me, dst,
        )

    def piece(i, o):
        return rows(i * cowners + o, cchunk)

    def c1(src, dst, o):
        return remote(cross_ref.at[piece(dst, o)], cbuf.at[src, o], c1_send.at[dst, o], c1_recv.at[src, o], mo * ni + dst, mc)

    def c2(src, dst):
        return remote(partial.at[dst], outer_buf.at[src], c2_send.at[dst], c2_recv.at[src], dst * ni + mi, mc)

    def ca(owner, dst):
        return remote(cown, cfull.at[piece(mi, owner)], ca_send.at[dst], ca_recv.at[owner], dst * ni + mi, mc)

    def cf(src, dst, o, ref):
        return remote(ref, cfull.at[piece(src, o)], cf_send.at[dst, o], cf_recv.at[src, o], mo * ni + dst, mc)

    peers(lambda p: owned(gowners, p, lambda: gs(me, p).start()))

    get_slab.wait()
    cross_ref[...] = jnp.zeros_like(cross_ref)

    def cross_step(t, _):
        at = pl.ds(pl.multiple_of(t * tile, tile), tile)
        cross_ref[...] += lax.dot_general(panel_ref[at, :], slab_ref[at, :], contract, preferred_element_type=jnp.float32)
        return 0

    lax.fori_loop(0, height // tile, cross_step, 0)
    cross_ref[...] *= scale

    def sum_gram():
        gown[...] = gram_ref[rows(me, gchunk), :]

        def add(p):
            gs(p, me).wait_recv()
            gown[...] += gbuf[p]

        sources(add)
        gfull[grows(me, mc), :] = gown[...]
        peers(lambda p: ga(me, p).start())
        cols(lambda q: remote(
            gown, gfull.at[grows(me, mc)], fw_send.at[me, q], fw_recv.at[me, mc], me, q).start())

    owned(gowners, me, sum_gram)
    pieces(lambda o: inner(lambda i: c1(mi, i, o).start()))

    def relay(p):
        def go():
            ga(p, me).wait_recv()
            cols(lambda q: fw(p, mc, q).start())

        owned(gowners, p, go)

    sources(relay)

    def relayed(q):
        def each(o, _):
            fw(o, q, mc).wait_recv()
            return 0

        lax.fori_loop(0, gowners, each, 0)

    cols(relayed)

    h = order // 2
    def sum_inner():
        def one(o):
            partial[o] = cross_ref[piece(mi, o), :]

            def add(i):
                c1(i, mi, o).wait_recv()
                partial[o] += cbuf[i, o]

            inner(add)
            pl.when(o != mo)(lambda: c2(mo, o).start())

        pieces(one)

    def relay_inner():
        def one(o):
            def go():
                ca(o, mo).wait_recv()
                inner(lambda i: cf(mi, i, o, cfull.at[piece(mi, o)]).start())

            owned_outer(o, go)

        outer(one)

    def owned_outer(o, body):
        if cowners == no:
            body()
        else:
            pl.when(o < cowners)(body)

    eliminate(gfull[:h, :h], r_ref, w_ref, sum_inner)
    w1 = w_ref[...]
    factor_ref[:h, :h] = r_ref[...]
    invt_ref[:h, :h] = w1
    r12 = mm(w1, gfull[:h, h:])
    factor_ref[:h, h:] = r12
    factor_ref[h:, :h] = jnp.zeros((h, h), jnp.float32)
    invt_ref[:h, h:] = jnp.zeros((h, h), jnp.float32)
    lower = gfull[h:, h:] - mm(r12, r12, 0, 0)

    def sum_outer():
        cown[...] = partial[mo]

        def add(o):
            c2(o, mo).wait_recv()
            cown[...] += outer_buf[o]

        outer(add)
        cfull[piece(mi, mo), :] = cown[...]
        outer(lambda o: ca(mo, o).start())
        inner(lambda i: cf(mi, i, mo, cown).start())

    owned_outer(mo, sum_outer)

    eliminate(lower, r_ref, w_ref, relay_inner)
    w2 = w_ref[...]
    factor_ref[h:, h:] = r_ref[...]
    invt_ref[h:, h:] = w2
    invt_ref[h:, :h] = -mm(w2, mm(r12, w1, 0, 0))

    pieces(lambda o: inner(lambda i: cf(i, mi, o, cown).wait_recv()))
    full_ref[...] = cfull[...]
    peers(lambda p: owned(gowners, p, lambda: gs(me, p).wait_send()))
    pieces(lambda o: inner(lambda i: c1(mi, i, o).wait_send()))
    pieces(lambda o: pl.when(o != mo)(lambda: c2(mo, o).wait_send()))
    pieces(lambda o: inner(lambda i: cf(mi, i, o, cown).wait_send()))
    owned(gowners, me, lambda: peers(lambda p: ga(me, p).wait_send()))
    owned_outer(mo, lambda: outer(lambda o: ca(mo, o).wait_send()))

    def sent(q):
        def each(o, _):
            fw(o, mc, q).wait_send()
            return 0

        lax.fori_loop(0, gowners, each, 0)

    cols(sent)


def sums_and_factor(panel, slab, n, ncol):
    height, order = panel.shape
    width = slab.shape[1]
    part = order // ncol
    scale = 1.0 / (height * n)
    gchunk = max(8, part // n)
    ni = 1
    while 4 * ni * ni <= n and n % (2 * ni) == 0:
        ni *= 2
    no = n // ni
    cowners = min(no, order // ni // 8)
    cchunk = order // ni // cowners
    f32 = jnp.float32
    dma = pltpu.SemaphoreType.DMA
    square = jax.ShapeDtypeStruct((order, order), f32)
    h = order // 2
    return pl.pallas_call(
        functools.partial(fused_kernel, n, ni, ncol, scale),
        out_shape=(square, square, jax.ShapeDtypeStruct((order, width), f32)),
        in_specs=[pl.BlockSpec(memory_space=pl.ANY)] * 2,
        out_specs=[pl.BlockSpec(memory_space=pltpu.VMEM)] * 3,
        scratch_shapes=[
            pltpu.VMEM(panel.shape, panel.dtype),
            pltpu.VMEM(slab.shape, slab.dtype),
            dma, dma,
            pltpu.VMEM((part, order), f32),
            pltpu.VMEM((order, width), f32),
            pltpu.VMEM((n, gchunk, order), f32),
            pltpu.VMEM((ni, cowners, cchunk, width), f32),
            pltpu.VMEM((cowners, cchunk, width), f32),
            pltpu.VMEM((no, cchunk, width), f32),
            pltpu.VMEM((order, order), f32),
            pltpu.VMEM((order, width), f32),
            pltpu.VMEM((gchunk, order), f32),
            pltpu.VMEM((cchunk, width), f32),
            pltpu.VMEM((h, h), f32),
            pltpu.VMEM((h, h), f32),
            dma((n,)), dma((n,)), dma((n,)), dma((n,)),
            dma((n, ncol)), dma((n, ncol)),
            dma((ni, cowners)), dma((ni, cowners)), dma((no,)), dma((no,)),
            dma((no,)), dma((no,)), dma((ni, cowners)), dma((ni, cowners)),
        ],
        compiler_params=pltpu.CompilerParams(collective_id=0, has_side_effects=True),
        name="sums_and_factor",
    )(panel, slab)


def finish_kernel(
    tiles, factor_ref, invt_ref, cross_ref, panel_hbm, slab_hbm, part_ref, coupling_hbm, out_hbm,
    panel_ref, slab_ref, out_ref, coupling_ref, panel_sem, slab_sem, out_sem, coupling_sem,
):
    tile = panel_ref.shape[0] // tiles
    rows = [pl.ds(t * tile, tile) for t in range(tiles)]
    get_panel = [pltpu.make_async_copy(panel_hbm.at[rows[t]], panel_ref.at[rows[t]], panel_sem.at[t]) for t in range(tiles)]
    get_slab = [pltpu.make_async_copy(slab_hbm.at[rows[t]], slab_ref.at[rows[t]], slab_sem.at[t]) for t in range(tiles)]
    put_out = [pltpu.make_async_copy(out_ref.at[rows[t]], out_hbm.at[rows[t]], out_sem.at[t]) for t in range(tiles)]
    put_coupling = pltpu.make_async_copy(coupling_ref, coupling_hbm, coupling_sem)
    for t in range(tiles):
        get_panel[t].start()
        get_slab[t].start()
    share = part_ref.shape[1]
    for q in range(factor_ref.shape[1] // share):

        @pl.when(lax.axis_index("col") == q)
        def _(q=q):
            part_ref[...] = factor_ref[:, q * share : (q + 1) * share]

    invt = invt_ref[...]
    coupling = mm(invt, cross_ref[...])
    coupling_ref[...] = coupling
    put_coupling.start()
    update = mm(invt, coupling, 0, 0).astype(jnp.bfloat16)
    for t in range(tiles):
        get_panel[t].wait()
        get_slab[t].wait()
        product = jnp.dot(panel_ref[rows[t], :], update, preferred_element_type=jnp.float32)
        out_ref[rows[t], :] = (slab_ref[rows[t], :].astype(jnp.float32) - product).astype(jnp.bfloat16)
        put_out[t].start()
    for t in range(tiles):
        put_out[t].wait()
    put_coupling.wait()


def finish(factor, invt, cross, panel, slab, ncol):
    order, width = cross.shape
    tiles = 8
    vmem, hbm = pl.BlockSpec(memory_space=pltpu.VMEM), pl.BlockSpec(memory_space=pl.ANY)
    dma = pltpu.SemaphoreType.DMA
    return pl.pallas_call(
        functools.partial(finish_kernel, tiles),
        out_shape=(
            jax.ShapeDtypeStruct((order, order // ncol), jnp.float32),
            jax.ShapeDtypeStruct((order, width), jnp.float32),
            jax.ShapeDtypeStruct(slab.shape, slab.dtype),
        ),
        in_specs=[vmem, vmem, vmem, hbm, hbm],
        out_specs=(vmem, hbm, hbm),
        scratch_shapes=[
            pltpu.VMEM(panel.shape, panel.dtype),
            pltpu.VMEM(slab.shape, slab.dtype),
            pltpu.VMEM(slab.shape, slab.dtype),
            pltpu.VMEM((order, width), jnp.float32),
            dma((tiles,)), dma((tiles,)), dma((tiles,)), dma,
        ],
        name="finish",
    )(factor, invt, cross, panel, slab)


def on_device(panel, slab):
    n, ncol = lax.axis_size("row"), lax.axis_size("col")
    factor, invt, cross = sums_and_factor(panel, slab, n, ncol)
    return finish(factor, invt, cross, panel, slab, ncol)


def solution(mesh):
    return jax.shard_map(
        on_device,
        mesh=mesh,
        in_specs=(P("row", None), P("row", "col")),
        out_specs=(P(None, "col"), P(None, "col"), P("row", "col")),
        check_vma=False,
    )
```

```python
import functools

import jax
import jax.numpy as jnp
from jax import lax
from jax.experimental import pallas as pl
from jax.experimental.pallas import tpu as pltpu
from jax.sharding import PartitionSpec as P

HI = lax.Precision.HIGHEST


def mm(a, b, ca=1, cb=0):
    return lax.dot_general(a, b, (((ca,), (cb,)), ((), ())), precision=HI, preferred_element_type=jnp.float32)


def split(x):
    high = x.astype(jnp.bfloat16).astype(jnp.float32)
    mid = (x - high).astype(jnp.bfloat16).astype(jnp.float32)
    return high, mid, x - high - mid


def eliminate(block, r_ref, w_ref, midway):
    n = block.shape[0]
    groups = n // 8
    lane = lax.broadcasted_iota(jnp.int32, (8, n), 1)
    sub = lax.broadcasted_iota(jnp.int32, (8, n), 0)
    a = [block[8 * t : 8 * t + 8, :] for t in range(groups)]
    w = [jnp.where(lane == sub + 8 * t, 1.0, 0.0).astype(jnp.float32) for t in range(groups)]

    def group(g, carry):
        a, w = list(carry[0]), list(carry[1])
        top, wtop = a[0], w[0]
        cols = [jnp.broadcast_to(top[:, j : j + 1], (8, n)) for j in range(8)]
        scale = jnp.zeros((8, n), jnp.float32)
        for j in range(8):
            inv = lax.rsqrt(jnp.broadcast_to(cols[j][j : j + 1, :], (8, n)))
            scale = jnp.where(sub == j, inv, scale)
            m = jnp.where(sub > j, cols[j], 0.0) * inv * inv
            for i in range(j + 1, 8):
                cols[i] = cols[i] - m * jnp.broadcast_to(cols[i][j : j + 1, :], (8, n))
            top = top - m * jnp.broadcast_to(top[j : j + 1, :], (8, n))
            wtop = wtop - m * jnp.broadcast_to(wtop[j : j + 1, :], (8, n))
        top, wtop = top * scale, wtop * scale
        start = pl.multiple_of(8 * g, 8)
        r_ref[pl.ds(start, 8), :] = jnp.where(lane >= sub + 8 * g, pltpu.roll(top, 8 * g, 1), 0.0)
        w_ref[pl.ds(start, 8), :] = wtop
        high, mid, low = split(jnp.concatenate([top, wtop], axis=1))
        left = jnp.concatenate([x[:, :n] for x in (high, high, mid, mid, high, low)], axis=0).astype(jnp.bfloat16)
        right = jnp.concatenate([high, mid, high, mid, low, high], axis=0).astype(jnp.bfloat16)
        u = lax.dot_general(left, right, (((0,), (0,)), ((), ())), preferred_element_type=jnp.float32)
        zero = jnp.zeros((8, n), jnp.float32)
        a = [pltpu.roll(a[t] - u[8 * t : 8 * t + 8, :n], n - 8, 1) for t in range(1, groups)] + [zero]
        w = [w[t] - u[8 * t : 8 * t + 8, n:] for t in range(1, groups)] + [zero]
        return tuple(a), tuple(w)

    carry = lax.fori_loop(0, groups // 2, group, (tuple(a), tuple(w)))
    midway()
    lax.fori_loop(groups // 2, groups, group, carry)


def fused_kernel(
    n, ni, ncol, scale, panel_hbm, slab_hbm, factor_ref, invt_ref, full_ref,
    panel_ref, slab_ref, panel_sem, slab_sem, gram_ref, cross_ref, gbuf, cbuf, partial, outer_buf, gfull, cfull, gown, cown, r_ref, w_ref,
    gs_send, gs_recv, ga_send, ga_recv, fw_send, fw_recv, c1_send, c1_recv, c2_send, c2_recv, ca_send, ca_recv, cf_send, cf_recv,
):
    me, mc = lax.axis_index("row"), lax.axis_index("col")
    get_panel = pltpu.make_async_copy(panel_hbm, panel_ref, panel_sem)
    get_panel.start()
    get_slab = pltpu.make_async_copy(slab_hbm, slab_ref, slab_sem)
    get_slab.start()
    order = gram_ref.shape[1]
    part = gram_ref.shape[0]
    gchunk, cchunk = gown.shape[0], cown.shape[0]
    gowners, cowners = part // gchunk, order // ni // cchunk
    no = n // ni
    mo, mi = me // ni, lax.rem(me, ni)

    def outer(body):
        def step(k, _):
            body(lax.rem(mo + k, no))
            return 0

        lax.fori_loop(1, no, step, 0)

    def inner(body):
        def step(k, _):
            body(lax.rem(mi + k, ni))
            return 0

        lax.fori_loop(1, ni, step, 0)

    def pieces(body):
        def step(k, _):
            body(lax.rem(mo + 1 + k, cowners))
            return 0

        lax.fori_loop(0, cowners, step, 0)

    def peers(body):
        def step(k, _):
            body(lax.rem(me + k, n))
            return 0

        lax.fori_loop(1, n, step, 0)

    def sources(body):
        def step(k, _):
            body(lax.rem(me + n - k, n))
            return 0

        lax.fori_loop(1, n, step, 0)

    def cols(body):
        def step(k, _):
            body(lax.rem(mc + k, ncol))
            return 0

        lax.fori_loop(1, ncol, step, 0)

    def owned(owners, who, body):
        if owners == n:
            body()
        else:
            pl.when(who < owners)(body)

    def remote(src, dst, send, recv, row, col):
        return pltpu.make_async_remote_copy(
            src_ref=src, dst_ref=dst, send_sem=send, recv_sem=recv,
            device_id={"row": row, "col": col}, device_id_type=pl.DeviceIdType.MESH,
        )

    barrier = pltpu.get_barrier_semaphore()
    peers(lambda p: pl.semaphore_signal(barrier, inc=1, device_id={"row": p, "col": mc}, device_id_type=pl.DeviceIdType.MESH))
    cols(lambda q: pl.semaphore_signal(barrier, inc=1, device_id={"row": me, "col": q}, device_id_type=pl.DeviceIdType.MESH))
    height = panel_ref.shape[0]
    tile = height // 4
    contract = (((0,), (0,)), ((), ()))
    get_panel.wait()
    for q in range(ncol):

        @pl.when(mc == q)
        def _(q=q):
            gram_ref[...] = jnp.zeros_like(gram_ref)

            def gram_step(t, _):
                at = pl.ds(pl.multiple_of(t * tile, tile), tile)
                gram_ref[...] += lax.dot_general(
                    panel_ref[at, q * part : (q + 1) * part], panel_ref[at, :], contract, preferred_element_type=jnp.float32
                )
                return 0

            lax.fori_loop(0, height // tile, gram_step, 0)

    gram_ref[...] *= scale
    pl.semaphore_wait(barrier, n + ncol - 2)

    def rows(owner, chunk):
        return pl.ds(pl.multiple_of(owner * chunk, 8), chunk)

    def grows(owner, col):
        return pl.ds(pl.multiple_of(col * part + owner * gchunk, 8), gchunk)

    def gs(src, dst):
        return remote(gram_ref.at[rows(dst, gchunk)], gbuf.at[src], gs_send.at[dst], gs_recv.at[src], dst, mc)

    def ga(owner, dst):
        return remote(gown, gfull.at[grows(owner, mc)], ga_send.at[dst], ga_recv.at[owner], dst, mc)

    def fw(owner, col, dst):
        return remote(
            gfull.at[grows(owner, col)], gfull.at[grows(owner, col)],
            fw_send.at[owner, dst], fw_recv.at[owner, col], me, dst,
        )

    def piece(i, o):
        return rows(i * cowners + o, cchunk)

    def c1(src, dst, o):
        return remote(cross_ref.at[piece(dst, o)], cbuf.at[src, o], c1_send.at[dst, o], c1_recv.at[src, o], mo * ni + dst, mc)

    def c2(src, dst):
        return remote(partial.at[dst], outer_buf.at[src], c2_send.at[dst], c2_recv.at[src], dst * ni + mi, mc)

    def ca(owner, dst):
        return remote(cown, cfull.at[piece(mi, owner)], ca_send.at[dst], ca_recv.at[owner], dst * ni + mi, mc)

    def cf(src, dst, o, ref):
        return remote(ref, cfull.at[piece(src, o)], cf_send.at[dst, o], cf_recv.at[src, o], mo * ni + dst, mc)

    peers(lambda p: owned(gowners, p, lambda: gs(me, p).start()))

    get_slab.wait()
    cross_ref[...] = jnp.zeros_like(cross_ref)

    def cross_step(t, _):
        at = pl.ds(pl.multiple_of(t * tile, tile), tile)
        cross_ref[...] += lax.dot_general(panel_ref[at, :], slab_ref[at, :], contract, preferred_element_type=jnp.float32)
        return 0

    lax.fori_loop(0, height // tile, cross_step, 0)
    cross_ref[...] *= scale

    def sum_gram():
        gown[...] = gram_ref[rows(me, gchunk), :]

        def add(p):
            gs(p, me).wait_recv()
            gown[...] += gbuf[p]

        sources(add)
        gfull[grows(me, mc), :] = gown[...]
        peers(lambda p: ga(me, p).start())
        cols(lambda q: remote(
            gown, gfull.at[grows(me, mc)], fw_send.at[me, q], fw_recv.at[me, mc], me, q).start())

    owned(gowners, me, sum_gram)
    pieces(lambda o: inner(lambda i: c1(mi, i, o).start()))

    def relay(p):
        def go():
            ga(p, me).wait_recv()
            cols(lambda q: fw(p, mc, q).start())

        owned(gowners, p, go)

    sources(relay)

    def relayed(q):
        def each(o, _):
            fw(o, q, mc).wait_recv()
            return 0

        lax.fori_loop(0, gowners, each, 0)

    cols(relayed)

    h = order // 2
    def sum_inner():
        def one(o):
            partial[o] = cross_ref[piece(mi, o), :]

            def add(i):
                c1(i, mi, o).wait_recv()
                partial[o] += cbuf[i, o]

            inner(add)
            pl.when(o != mo)(lambda: c2(mo, o).start())

        pieces(one)

    def relay_inner():
        def one(o):
            def go():
                ca(o, mo).wait_recv()
                inner(lambda i: cf(mi, i, o, cfull.at[piece(mi, o)]).start())

            owned_outer(o, go)

        outer(one)

    def owned_outer(o, body):
        if cowners == no:
            body()
        else:
            pl.when(o < cowners)(body)

    eliminate(gfull[:h, :h], r_ref, w_ref, sum_inner)
    w1 = w_ref[...]
    factor_ref[:h, :h] = r_ref[...]
    invt_ref[:h, :h] = w1
    r12 = mm(w1, gfull[:h, h:])
    factor_ref[:h, h:] = r12
    factor_ref[h:, :h] = jnp.zeros((h, h), jnp.float32)
    invt_ref[:h, h:] = jnp.zeros((h, h), jnp.float32)
    lower = gfull[h:, h:] - mm(r12, r12, 0, 0)

    def sum_outer():
        cown[...] = partial[mo]

        def add(o):
            c2(o, mo).wait_recv()
            cown[...] += outer_buf[o]

        outer(add)
        cfull[piece(mi, mo), :] = cown[...]
        outer(lambda o: ca(mo, o).start())
        inner(lambda i: cf(mi, i, mo, cown).start())

    owned_outer(mo, sum_outer)

    eliminate(lower, r_ref, w_ref, relay_inner)
    w2 = w_ref[...]
    factor_ref[h:, h:] = r_ref[...]
    invt_ref[h:, h:] = w2
    invt_ref[h:, :h] = -mm(w2, mm(r12, w1, 0, 0))

    pieces(lambda o: inner(lambda i: cf(i, mi, o, cown).wait_recv()))
    full_ref[...] = cfull[...]
    peers(lambda p: owned(gowners, p, lambda: gs(me, p).wait_send()))
    pieces(lambda o: inner(lambda i: c1(mi, i, o).wait_send()))
    pieces(lambda o: pl.when(o != mo)(lambda: c2(mo, o).wait_send()))
    pieces(lambda o: inner(lambda i: cf(mi, i, o, cown).wait_send()))
    owned(gowners, me, lambda: peers(lambda p: ga(me, p).wait_send()))
    owned_outer(mo, lambda: outer(lambda o: ca(mo, o).wait_send()))

    def sent(q):
        def each(o, _):
            fw(o, mc, q).wait_send()
            return 0

        lax.fori_loop(0, gowners, each, 0)

    cols(sent)


def sums_and_factor(panel, slab, n, ncol):
    height, order = panel.shape
    width = slab.shape[1]
    part = order // ncol
    scale = 1.0 / (height * n)
    gchunk = max(8, part // n)
    ni = 1
    while 4 * ni * ni <= n and n % (2 * ni) == 0:
        ni *= 2
    no = n // ni
    cowners = min(no, order // ni // 8)
    cchunk = order // ni // cowners
    f32 = jnp.float32
    dma = pltpu.SemaphoreType.DMA
    square = jax.ShapeDtypeStruct((order, order), f32)
    h = order // 2
    return pl.pallas_call(
        functools.partial(fused_kernel, n, ni, ncol, scale),
        out_shape=(square, square, jax.ShapeDtypeStruct((order, width), f32)),
        in_specs=[pl.BlockSpec(memory_space=pl.ANY)] * 2,
        out_specs=[pl.BlockSpec(memory_space=pltpu.VMEM)] * 3,
        scratch_shapes=[
            pltpu.VMEM(panel.shape, panel.dtype),
            pltpu.VMEM(slab.shape, slab.dtype),
            dma, dma,
            pltpu.VMEM((part, order), f32),
            pltpu.VMEM((order, width), f32),
            pltpu.VMEM((n, gchunk, order), f32),
            pltpu.VMEM((ni, cowners, cchunk, width), f32),
            pltpu.VMEM((cowners, cchunk, width), f32),
            pltpu.VMEM((no, cchunk, width), f32),
            pltpu.VMEM((order, order), f32),
            pltpu.VMEM((order, width), f32),
            pltpu.VMEM((gchunk, order), f32),
            pltpu.VMEM((cchunk, width), f32),
            pltpu.VMEM((h, h), f32),
            pltpu.VMEM((h, h), f32),
            dma((n,)), dma((n,)), dma((n,)), dma((n,)),
            dma((n, ncol)), dma((n, ncol)),
            dma((ni, cowners)), dma((ni, cowners)), dma((no,)), dma((no,)),
            dma((no,)), dma((no,)), dma((ni, cowners)), dma((ni, cowners)),
        ],
        compiler_params=pltpu.CompilerParams(collective_id=0, has_side_effects=True),
        name="sums_and_factor",
    )(panel, slab)


def finish_kernel(
    tiles, factor_ref, invt_ref, cross_ref, panel_hbm, slab_hbm, part_ref, coupling_hbm, out_hbm,
    panel_ref, slab_ref, out_ref, coupling_ref, panel_sem, slab_sem, out_sem, coupling_sem,
):
    tile = panel_ref.shape[0] // tiles
    rows = [pl.ds(t * tile, tile) for t in range(tiles)]
    get_panel = [pltpu.make_async_copy(panel_hbm.at[rows[t]], panel_ref.at[rows[t]], panel_sem.at[t]) for t in range(tiles)]
    get_slab = [pltpu.make_async_copy(slab_hbm.at[rows[t]], slab_ref.at[rows[t]], slab_sem.at[t]) for t in range(tiles)]
    put_out = [pltpu.make_async_copy(out_ref.at[rows[t]], out_hbm.at[rows[t]], out_sem.at[t]) for t in range(tiles)]
    put_coupling = pltpu.make_async_copy(coupling_ref, coupling_hbm, coupling_sem)
    for t in range(tiles):
        get_panel[t].start()
        get_slab[t].start()
    share = part_ref.shape[1]
    for q in range(factor_ref.shape[1] // share):

        @pl.when(lax.axis_index("col") == q)
        def _(q=q):
            part_ref[...] = factor_ref[:, q * share : (q + 1) * share]

    invt = invt_ref[...]
    coupling = mm(invt, cross_ref[...])
    coupling_ref[...] = coupling
    put_coupling.start()
    update = mm(invt, coupling, 0, 0).astype(jnp.bfloat16)
    for t in range(tiles):
        get_panel[t].wait()
        get_slab[t].wait()
        product = jnp.dot(panel_ref[rows[t], :], update, preferred_element_type=jnp.float32)
        out_ref[rows[t], :] = (slab_ref[rows[t], :].astype(jnp.float32) - product).astype(jnp.bfloat16)
        put_out[t].start()
    for t in range(tiles):
        put_out[t].wait()
    put_coupling.wait()


def finish(factor, invt, cross, panel, slab, ncol):
    order, width = cross.shape
    tiles = 8
    vmem, hbm = pl.BlockSpec(memory_space=pltpu.VMEM), pl.BlockSpec(memory_space=pl.ANY)
    dma = pltpu.SemaphoreType.DMA
    return pl.pallas_call(
        functools.partial(finish_kernel, tiles),
        out_shape=(
            jax.ShapeDtypeStruct((order, order // ncol), jnp.float32),
            jax.ShapeDtypeStruct((order, width), jnp.float32),
            jax.ShapeDtypeStruct(slab.shape, slab.dtype),
        ),
        in_specs=[vmem, vmem, vmem, hbm, hbm],
        out_specs=(vmem, hbm, hbm),
        scratch_shapes=[
            pltpu.VMEM(panel.shape, panel.dtype),
            pltpu.VMEM(slab.shape, slab.dtype),
            pltpu.VMEM(slab.shape, slab.dtype),
            pltpu.VMEM((order, width), jnp.float32),
            dma((tiles,)), dma((tiles,)), dma((tiles,)), dma,
        ],
        name="finish",
    )(factor, invt, cross, panel, slab)


def on_device(panel, slab):
    n, ncol = lax.axis_size("row"), lax.axis_size("col")
    factor, invt, cross = sums_and_factor(panel, slab, n, ncol)
    return finish(factor, invt, cross, panel, slab, ncol)


def solution(mesh):
    return jax.shard_map(
        on_device,
        mesh=mesh,
        in_specs=(P("row", None), P("row", "col")),
        out_specs=(P(None, "col"), P(None, "col"), P("row", "col")),
        check_vma=False,
    )
```
